32 devices in a mesh: dp: 16 (over z, y, x), tensor: 2 (over core).
Axes of the slice: x: 2, y: 2, z: 4, core: 2. Of those that a mesh axis runs over, the one named last changes fastest.
Arguments:
- tokens_in: bfloat16 [4096, 1536], P('dp'), may hold values from -6 to 6
- seq_lengths: int32 [16, 16], P('dp'), may hold values from 0 to 256, as said below
- gain_attn: bfloat16 [1536], P('dp'), may hold values from 0.099609375 to 1.8984375
- w_query: bfloat16 [1536, 1536], P(('tensor', 'dp')), may hold values from -3 to 3
- b_query: bfloat16 [1536], P(('tensor', 'dp')), may hold values from -3 to 3
- w_key: bfloat16 [256, 1536], P(('tensor', 'dp')), may hold values from -3 to 3
- b_key: bfloat16 [256], P(('tensor', 'dp')), may hold values from -3 to 3
- w_value: bfloat16 [256, 1536], P(('tensor', 'dp')), may hold values from -0.15625 to 0.15625
- b_value: bfloat16 [256], P(('tensor', 'dp')), may hold values from -3 to 3
- w_out: bfloat16 [1536, 1536], P(('tensor', 'dp')), may hold values from -0.625 to 0.625
- gain_mlp: bfloat16 [1536], P('dp'), may hold values from 0.099609375 to 1.8984375
- w_gate: bfloat16 [8960, 1536], P(('tensor', 'dp')), may hold values from -0.15625 to 0.15625
- w_up: bfloat16 [8960, 1536], P(('tensor', 'dp')), may hold values from -0.15625 to 0.15625
- w_down: bfloat16 [8960, 1536], P(('tensor', 'dp')), may hold values from -0.125 to 0.125
- grad_out: bfloat16 [4096, 1536], P('dp'), may hold values from -6 to 6
Outputs:
- block_out: float32 [4096, 1536], P('dp')
- grad_in: float32 [4096, 1536], P('dp')
- grad_gain_attn: float32 [1536], P('dp')
- grad_w_query: float32 [1536, 1536], P(('tensor', 'dp'))
- grad_b_query: float32 [1536], P(('tensor', 'dp'))
- grad_w_key: float32 [256, 1536], P(('tensor', 'dp'))
- grad_b_key: float32 [256], P('tensor')
- grad_w_value: float32 [256, 1536], P(('tensor', 'dp'))
- grad_b_value: float32 [256], P(('tensor', 'dp'))
- grad_w_out: float32 [1536, 1536], P(('tensor', 'dp'))
- grad_gain_mlp: float32 [1536], P('dp')
- grad_w_gate: float32 [8960, 1536], P(('tensor', 'dp'))
- grad_w_up: float32 [8960, 1536], P(('tensor', 'dp'))
- grad_w_down: float32 [8960, 1536], P(('tensor', 'dp'))
The draws below stay inside these ranges and needn't reach their ends.
Inputs may be any that keep to these rules, and one draw needn't show every extreme that they name: `seq_lengths`: row r lists, in order, the lengths of the sequences packed in tokens r * 256 to (r + 1) * 256 - 1: they sum to 256, live slots come first and are 1 or more, unused slots are 0, and some row holds a single sequence of 256 tokens.
All inputs are finite; a program needn't handle non-finite values.
Results may differ from the reference program's by a relative error of at most 0.023.
Values may be sent and summed in bfloat16 or wider, within the bound.
No kernel may reach another device: no remote copies, remote signals or barrier semaphores. Data moves between devices by JAX's collectives and lax.ppermute only.
A program may use at most 256 MiB of HBM per device.

```python
import math
import jax
import jax.numpy as jnp
from jax import lax

D = 1536
H = 12
KVH = 2
HD = 128
FF = 8960
TOK_DEV = 256
SLOTS = 16
NTOK = 4096
N_DP = 16


def draw_tokens_in(key, part):
    base_key = jax.random.fold_in(key, 21)
    result = jnp.clip(jax.random.normal(base_key, (NTOK, D), jnp.float32), -6.0, 6.0)
    return result.astype(jnp.bfloat16)


def draw_seq_lengths(key, part):
    exponents = jax.random.randint(jax.random.fold_in(key, 4), (N_DP,), 0, 5)
    counts_all = jnp.left_shift(jnp.ones_like(exponents), exponents)
    chosen = jax.random.randint(jax.random.fold_in(key, 5), (), 0, N_DP)
    counts_all = jnp.where(jnp.arange(N_DP) == chosen, 1, counts_all)
    row_keys = jax.random.split(jax.random.fold_in(key, 3), N_DP)

    def one_row(row_key, seq_count):
        ordering = jax.random.permutation(row_key, TOK_DEV - 1)[:SLOTS - 1] + 1
        live_slots = jnp.arange(SLOTS - 1) < seq_count - 1
        cut_points = jnp.sort(jnp.where(live_slots, ordering, TOK_DEV)).astype(jnp.int32)
        bounds = jnp.concatenate([jnp.zeros((1,), jnp.int32), cut_points, jnp.full((1,), TOK_DEV, jnp.int32)])
        return bounds[1:] - bounds[:-1]
    return jax.vmap(one_row)(row_keys, counts_all).astype(jnp.int32)


def projection_draw(key, rows_total, salt):
    sub_key = jax.random.fold_in(key, salt)
    result = jnp.clip(jax.random.normal(sub_key, (rows_total, D), jnp.float32), -6.0, 6.0) / math.sqrt(D)
    return result


def draw_w_query(key, part):
    return projection_draw(key, H * HD, 11).astype(jnp.bfloat16)


def draw_w_key(key, part):
    return projection_draw(key, KVH * HD, 12).astype(jnp.bfloat16)


def steps_of(own_key, dims, cuts, low, largest):
    def one(axis_at, shards_of):
        steps = jax.random.uniform(jax.random.fold_in(jax.random.fold_in(own_key, 6), axis_at), (shards_of,), jnp.float32, low / len(cuts), largest / len(cuts))
        return jnp.repeat(jnp.exp(steps), dims[axis_at] // shards_of).reshape((-1,) + (1,) * (len(dims) - axis_at - 1))

    factor_of = one(*cuts[0])
    for cut in cuts[1:]:
        factor_of = factor_of * one(*cut)
    return factor_of


def noise(stream_key, extent, scale, limit, cuts=(), kind=jnp.bfloat16):
    drawn = scale * jax.random.normal(stream_key, extent, jnp.float32)
    if cuts:
        drawn = drawn * steps_of(stream_key, extent, cuts, -0.22, 0.18)
    return jnp.clip(drawn, -limit, limit).astype(kind)


def setup_inputs(seed: int = 0) -> dict:
    arg_keys = jax.random.split(jax.random.key(seed), 16)
    tokens_in = draw_tokens_in(jax.random.fold_in(arg_keys[15], 71), 0)
    seq_lengths = draw_seq_lengths(jax.random.fold_in(arg_keys[15], 71), 0)
    gain_attn = jnp.clip(1.0 + 0.18 * jax.random.normal(arg_keys[2], (D,), jnp.float32), 0.099609375, 1.8984375).astype(jnp.bfloat16)
    w_query = draw_w_query(jax.random.fold_in(arg_keys[15], 71), 0)
    b_query = noise(arg_keys[4], (H * HD,), 0.5, 3.0, ((0, 32),))
    w_key = draw_w_key(jax.random.fold_in(arg_keys[15], 71), 0)
    b_key = noise(arg_keys[6], (KVH * HD,), 0.5, 3.0, ((0, 32),))
    w_value = noise(arg_keys[7], (KVH * HD, D), D ** -0.5, 0.15625, ((0, 32),))
    b_value = noise(arg_keys[8], (KVH * HD,), 0.5, 3.0, ((0, 32),))
    w_out = noise(arg_keys[9], (H * HD, D), (H * HD // 16) ** -0.5, 0.625, ((0, 32),))
    gain_mlp = jnp.clip(1.0 + 0.18 * jax.random.normal(arg_keys[10], (D,), jnp.float32), 0.099609375, 1.8984375).astype(jnp.bfloat16)
    w_gate = noise(arg_keys[11], (FF, D), D ** -0.5, 0.15625, ((0, 32),))
    w_up = noise(arg_keys[12], (FF, D), D ** -0.5, 0.15625, ((0, 32),))
    w_down = noise(arg_keys[13], (FF, D), (FF // 4) ** -0.5, 0.125, ((0, 32),))
    grad_out = noise(arg_keys[14], (NTOK, D), 1.0, 6.0, ((0, 16),))
    return {"tokens_in": tokens_in, "seq_lengths": seq_lengths, "gain_attn": gain_attn, "w_query": w_query, "b_query": b_query, "w_key": w_key, "b_key": b_key, "w_value": w_value, "b_value": b_value, "w_out": w_out, "gain_mlp": gain_mlp, "w_gate": w_gate, "w_up": w_up, "w_down": w_down, "grad_out": grad_out}


EPSILON = 1e-06
ROPE_BASE = 1000000.0
HIGHEST = lax.Precision.HIGHEST

@jax.custom_vjp
def low(v):
    return lax.optimization_barrier(v.astype(jnp.bfloat16)).astype(jnp.float32)

@jax.custom_vjp
def low_back(v):
    return v

def low_keep(v):
    return (low(v), None)

def low_pass(kept, grad):
    return (grad,)

def back_keep(v):
    return (v, None)

def back_low(kept, grad):
    return (low(grad),)
low.defvjp(low_keep, low_pass)
low_back.defvjp(back_keep, back_low)

def packed_layout(seq_lengths, row_tokens):
    ends_all = jnp.cumsum(seq_lengths, axis=1).astype(jnp.int32)
    places = jnp.arange(row_tokens, dtype=jnp.int32)
    passed = ends_all[:, None, :] <= places[None, :, None]
    segment = lax.optimization_barrier(jnp.sum(passed.astype(jnp.int32), axis=2)).astype(jnp.int32)
    opening = lax.optimization_barrier(jnp.sum(jnp.where(passed, seq_lengths[:, None, :], 0), axis=2)).astype(jnp.int32)
    return (segment, (places[None, :] - opening).astype(jnp.int32))

def rope_tables(positions):
    half_size = HD // 2
    frequency = ROPE_BASE ** (-(jnp.arange(half_size, dtype=jnp.float32) * 2.0) / HD)
    angles = positions.astype(jnp.float32)[:, None] * frequency[None, :]
    cosine = jnp.cos(angles)
    sine_table = jnp.sin(angles)
    return (jnp.concatenate([cosine, cosine], axis=1), jnp.concatenate([sine_table, sine_table], axis=1))

def rotate(vectors, cosine, sine_table):
    half_size = vectors.shape[-1] // 2
    turned = jnp.concatenate([-vectors[..., half_size:], vectors[..., :half_size]], axis=-1)
    return vectors * cosine[:, None, :] + turned * sine_table[:, None, :]

def inverse_rms(values):
    return lax.rsqrt(lax.optimization_barrier(jnp.mean(values * values, axis=1, keepdims=True)) + EPSILON)

def matmul(left_side, right_side):
    return jnp.dot(left_side, right_side, precision=HIGHEST)

def block_forward(inputs, gain_attn, w_query, b_query, w_key, b_key, w_value, b_value, w_out, gain_mlp, w_gate, w_up, w_down, segment, position):
    group_rows = 1
    for candidate in range(1, N_DP + 1):
        if N_DP % candidate == 0 and candidate * TOK_DEV <= 4096:
            group_rows = candidate
    group_count = N_DP // group_rows
    group_tokens = group_rows * TOK_DEV
    group_heads = H // KVH
    score_scale = 1.0 / math.sqrt(HD)
    places = jnp.arange(TOK_DEV, dtype=jnp.int32)

    def group_step(operands):
        x_group, seg_group, pos_group = operands
        cosine, sine_table = rope_tables(pos_group.reshape(group_tokens))
        first_low = low(x_group * inverse_rms(x_group) * gain_attn)
        query_pre = low_back(matmul(first_low, w_query.T) + b_query)
        keys_pre = low_back(matmul(first_low, w_key.T) + b_key)
        values_pre = low_back(low(matmul(first_low, w_value.T) + b_value))
        query_rot = low(rotate(query_pre.reshape(group_tokens, H, HD), cosine, sine_table))
        query_rot = query_rot.reshape(group_rows, TOK_DEV, KVH, group_heads, HD)
        keys_rot = low(rotate(keys_pre.reshape(group_tokens, KVH, HD), cosine, sine_table))
        keys_rot = keys_rot.reshape(group_rows, TOK_DEV, KVH, HD)
        values_low = values_pre.reshape(group_rows, TOK_DEV, KVH, HD)
        scores = low_back(jnp.einsum('rqkgd,rtkd->rkgqt', query_rot, keys_rot, precision=HIGHEST) * score_scale)
        allowed = (seg_group[:, :, None] == seg_group[:, None, :]) & (places[None, :, None] >= places[None, None, :])
        scores = jnp.where(allowed[:, None, None], scores, -jnp.inf)
        log_total = jax.nn.logsumexp(scores, axis=4, keepdims=True)
        probability = low(jnp.exp(scores - log_total))
        attended = low_back(low(jnp.einsum('rkgqt,rtkd->rqkgd', probability, values_low, precision=HIGHEST)))
        attended = attended.reshape(group_tokens, H * HD)
        hidden_state = x_group + low_back(matmul(attended, w_out))
        second_low = low(hidden_state * inverse_rms(hidden_state) * gain_mlp)
        gate_vals = low_back(matmul(second_low, w_gate.T))
        up_vals = low_back(matmul(second_low, w_up.T))
        hidden = low(jax.nn.silu(gate_vals) * up_vals)
        return hidden_state + low_back(matmul(hidden, w_down))
    pieces = (inputs.reshape(group_count, group_tokens, D), segment.reshape(group_count, group_rows, TOK_DEV), position.reshape(group_count, group_rows, TOK_DEV))
    return lax.map(jax.checkpoint(group_step), pieces).reshape(NTOK, D)

def reference(tokens_in, seq_lengths, gain_attn, w_query, b_query, w_key, b_key, w_value, b_value, w_out, gain_mlp, w_gate, w_up, w_down, grad_out):
    segment, position = packed_layout(seq_lengths, TOK_DEV)
    params = tuple((array_in.astype(jnp.float32) for array_in in (tokens_in, gain_attn, w_query, b_query, w_key, b_key, w_value, b_value, w_out, gain_mlp, w_gate, w_up, w_down)))

    def forward_only(*weights_all):
        return block_forward(*weights_all, segment, position)
    block_out, pullback = jax.vjp(forward_only, *params)
    gradients = pullback(grad_out.astype(jnp.float32))
    return (block_out, gradients[0], gradients[1], gradients[2], gradients[3], gradients[4], gradients[5], gradients[6], gradients[7], gradients[8], gradients[9], gradients[10], gradients[11], gradients[12])
```

```python
import math

import jax
import jax.numpy as jnp
from jax import lax
from jax.sharding import PartitionSpec as P

HD = 128
EPSILON = 1e-06
ROPE_BASE = 1000000.0
AXES = ("dp", "tensor")
BF = jnp.bfloat16
F32 = jnp.float32


def dims_of(n_dp):
    if n_dp == 16:
        return (4, 2, 2)
    if n_dp == 64:
        return (4, 4, 4)
    return (n_dp, 1, 1)


def make_rings(n_dp):
    n0, n1, n2 = dims_of(n_dp)
    same = n1 == n2

    def shifted(dp, axis):
        c = [dp // (n1 * n2), dp // n2 % n1, dp % n2]
        c[axis] = (c[axis] + 1) % (n0, n1, n2)[axis]
        return (c[0] * n1 + c[1]) * n2 + c[2]

    def ring(axis_core0, axis_core1):
        pairs = []
        for dp in range(n_dp):
            for core, axis in ((0, axis_core0), (1, axis_core1)):
                pairs.append((dp * 2 + core, shifted(dp, axis) * 2 + core))
        return pairs

    return {
        "z": (n0, ring(0, 0)),
        "a": (n2, ring(2, 1) if same else ring(2, 2)),
        "b": (n1, ring(1, 2) if same else ring(1, 1)),
        "t": (2, [(d * 2 + c, d * 2 + 1 - c) for d in range(n_dp) for c in (0, 1)]),
    }


def dot(a, b):
    return lax.dot_general(a, b, (((1,), (0,)), ((), ())), preferred_element_type=F32)


def dot_t(a, b):
    return lax.dot_general(a, b, (((1,), (1,)), ((), ())), preferred_element_type=F32)


def contract(a, b):
    return lax.dot_general(a, b, (((0,), (0,)), ((), ())), preferred_element_type=F32)


def inverse_rms(values):
    return lax.rsqrt(jnp.mean(values * values, axis=1, keepdims=True) + EPSILON)


def packed_layout(lengths, row_tokens):
    ends = jnp.cumsum(lengths)
    places = jnp.arange(row_tokens, dtype=jnp.int32)
    passed = ends[None, :] <= places[:, None]
    segment = jnp.sum(passed.astype(jnp.int32), axis=1)
    opening = jnp.sum(jnp.where(passed, lengths[None, :], 0), axis=1)
    return segment, places - opening


def rope_tables(positions):
    half = HD // 2
    frequency = ROPE_BASE ** (-(jnp.arange(half, dtype=F32) * 2.0) / HD)
    angles = positions.astype(F32)[:, None] * frequency[None, :]
    cosine, sine = jnp.cos(angles), jnp.sin(angles)
    return jnp.concatenate([cosine, cosine], axis=1), jnp.concatenate([sine, sine], axis=1)


def rotate(e, c, s):
    half = HD // 2
    return e * c + jnp.concatenate([-e[:, half:], e[:, :half]], axis=1) * s


def unrotate(g, c, s):
    half = HD // 2
    gs = g * s
    return g * c + jnp.concatenate([gs[:, half:], -gs[:, :half]], axis=1)


def by_head(m, heads):
    return jnp.concatenate([m[:, n * HD : (n + 1) * HD] for n in range(heads)], axis=0)


def side_by_side(m, heads, rows):
    return jnp.concatenate([m[n * rows : (n + 1) * rows] for n in range(heads)], axis=1)


def build(n_dp):
    rings = make_rings(n_dp)
    n0, n1, n2 = dims_of(n_dp)
    nz, na, nb = rings["z"][0], rings["a"][0], rings["b"][0]

    def shift(v, name):
        return lax.ppermute(v, AXES, rings[name][1])

    def gather(own):
        line = [own]
        for _ in range(nz - 1):
            line.append(shift(line[-1], "z"))
        planes = [line]
        for _ in range(na - 1):
            planes.append([shift(v, "a") for v in planes[-1]])
        cubes = [planes]
        for _ in range(nb - 1):
            cubes.append([[shift(v, "b") for v in row] for row in cubes[-1]])
        return cubes

    def ring_sum(parts, name):
        total = parts[1]
        for r in range(2, len(parts) + 1):
            total = shift(total.astype(BF), name).astype(F32) + parts[r % len(parts)]
        return total

    def scatter(blocks):
        planes = []
        for ra in range(na):
            planes.append(
                [
                    ring_sum([blocks[rb][ra][rz] for rb in range(nb)], "b") if nb > 1 else blocks[0][ra][rz]
                    for rz in range(nz)
                ]
            )
        line = [
            ring_sum([planes[ra][rz] for ra in range(na)], "a") if na > 1 else planes[0][rz]
            for rz in range(nz)
        ]
        return ring_sum(line, "z")

    def flat(blocks):
        return [v for plane in blocks for row in plane for v in row]

    def nest(items):
        it = iter(items)
        return [[[next(it) for _ in range(nz)] for _ in range(na)] for _ in range(nb)]

    def owners():
        me = lax.axis_index("dp")
        core = lax.axis_index("tensor")
        z, y, x = me // (n1 * n2), me // n2 % n1, me % n2
        a, b = (x, y) if n1 != n2 else (jnp.where(core == 0, x, y), jnp.where(core == 0, y, x))
        out = []
        for rb in range(nb):
            for ra in range(na):
                for rz in range(nz):
                    zz, aa, bb = (z - rz) % nz, (a - ra) % na, (b - rb) % nb
                    if n1 != n2:
                        yy, xx = bb, aa
                    else:
                        yy, xx = jnp.where(core == 0, bb, aa), jnp.where(core == 0, aa, bb)
                    out.append((zz * n1 + yy) * n2 + xx)
        return jnp.stack(out)

    def shards(
        tokens_in, seq_lengths, gain_attn, w_query, b_query, w_key, b_key, w_value, b_value, w_out,
        gain_mlp, w_gate, w_up, w_down, grad_out,
    ):
        rows, width = tokens_in.shape
        half = rows // 2
        core = lax.axis_index("tensor")
        scale = 1.0 / math.sqrt(HD)
        nq, nk, nv, no = w_query.shape[0], w_key.shape[0], w_value.shape[0], w_out.shape[0]
        ng = gain_attn.shape[0]
        q_all, k_all = nq * n_dp, nk * n_dp
        heads = q_all // HD
        units = w_gate.shape[0]
        mine_of = lambda v: lax.dynamic_slice_in_dim(v, core * half, half, 0)
        other_of = lambda v: lax.dynamic_slice_in_dim(v, (1 - core) * half, half, 0)

        def rejoin(mine):
            other = shift(mine, "t")
            return jnp.where(core == 0, jnp.concatenate([mine, other]), jnp.concatenate([other, mine]))

        small = jnp.concatenate([gain_attn, gain_mlp, b_query, b_key, b_value])
        n_small = small.shape[0]
        small_row = jnp.pad(small, (0, width - n_small))[None]
        qkv_own = jnp.concatenate([w_query, w_key, w_value, jnp.pad(small_row, ((0, 15), (0, 0)))], axis=0)
        n_qkv = nq + nk + nv
        qkv_blocks = flat(gather(qkv_own))
        out_blocks = flat(gather(w_out))
        go_own = mine_of(grad_out)
        go_blocks = gather(go_own)
        padded = -(-2 * units // 128) * 128

        def pair_rows(w):
            return jnp.concatenate([w, shift(w, "t"), jnp.zeros((padded - 2 * units, width), BF)], axis=0)

        wg, wu, wd = pair_rows(w_gate), pair_rows(w_up), pair_rows(w_down)
        wgu = jnp.concatenate([wg, wu], axis=0)

        owner = owners()
        f = jnp.arange(n_qkv * n_dp, dtype=jnp.int32)
        fb, fr = owner[f // n_qkv], f % n_qkv
        target = jnp.where(
            fr < nq,
            fb * nq + fr,
            jnp.where(fr < nq + nk, q_all + fb * nk + fr - nq, q_all + k_all + fb * nv + fr - nq - nk),
        )
        columns = jnp.arange(n_qkv * n_dp, dtype=jnp.int32)
        order_qkv = (columns[:, None] == target[None, :]).astype(BF)
        f = jnp.arange(no * n_dp, dtype=jnp.int32)
        target_o = owner[f // no] * no + f % no
        order_out = (jnp.arange(no * n_dp, dtype=jnp.int32)[:, None] == target_o[None, :]).astype(BF)
        order_small = (jnp.arange(n_dp)[:, None] == owner[None, :]).astype(BF)

        segment, position = packed_layout(seq_lengths[0], rows)
        cosine, sine = rope_tables(position)
        places = jnp.arange(rows, dtype=jnp.int32)
        allowed = (segment[:, None] == segment[None, :]) & (places[:, None] >= places[None, :])
        allowed = jnp.tile(allowed, (heads, 1))
        cos_all, sin_all = jnp.tile(cosine, (heads, 1)), jnp.tile(sine, (heads, 1))

        w_rel = jnp.concatenate([v[:n_qkv] for v in qkv_blocks], axis=0)
        w_abs = dot(order_qkv, w_rel).astype(BF)
        smalls = dot(order_small, jnp.concatenate([v[n_qkv : n_qkv + 1, :n_small] for v in qkv_blocks], axis=0))
        cut = [ng, 2 * ng, 2 * ng + nq, 2 * ng + nq + nk]
        gain1, gain2, bq, bk, bv = [v.reshape(-1) for v in jnp.split(smalls, cut, axis=1)]
        x = tokens_in.astype(F32)
        inv1 = inverse_rms(x)
        u1 = x * inv1
        a1 = (u1 * gain1).astype(BF)
        qkv = dot_t(a1, w_abs) + jnp.concatenate([bq, bk, bv])
        q6 = by_head(qkv[:, :q_all], heads)
        qr = rotate(q6, cos_all, sin_all).astype(BF)
        kr = rotate(qkv[:, q_all : q_all + k_all], cosine, sine).astype(BF)
        vr = qkv[:, q_all + k_all :].astype(BF)
        scores = jnp.where(allowed, dot_t(qr, kr) * scale, -jnp.inf)
        largest = jnp.max(scores, axis=1, keepdims=True)
        raised = jnp.exp(scores - largest)
        prob = raised / jnp.sum(raised, axis=1, keepdims=True)
        prob_low = prob.astype(BF)
        o6 = dot(prob_low, vr).astype(BF)
        attended = side_by_side(o6, heads, rows)
        o_rel = dot(attended, order_out).astype(BF)
        wo_rel = jnp.concatenate(out_blocks, axis=0)
        theirs = shift(dot(other_of(o_rel), wo_rel), "t")
        h = mine_of(x) + (dot(mine_of(o_rel), wo_rel) + theirs)
        inv2 = inverse_rms(h)
        u2 = h * inv2
        a2 = (u2 * gain2).astype(BF)

        a2_blocks = gather(a2)
        da2_parts, y_parts = [], []
        g_gu = g_d = None
        for rb in range(nb):
            X = jnp.concatenate([v for row in a2_blocks[rb] for v in row], axis=0)
            G = jnp.concatenate([v for row in go_blocks[rb] for v in row], axis=0)
            gu = dot_t(X, wgu)
            gate, up = gu[:, :padded], gu[:, padded:]
            g_hid = dot_t(G, wd)
            sig = jax.nn.sigmoid(gate)
            silu = gate * sig
            hidden = (silu * up).astype(BF)
            dgate = (g_hid * up * (sig * (1.0 + gate * (1.0 - sig)))).astype(BF)
            dup = (g_hid * silu).astype(BF)
            dgu = jnp.concatenate([dgate, dup], axis=1)
            da2_parts.append(dot(dgu, wgu))
            y_parts.append(dot(hidden, wd))
            part_gu, part_d = contract(dgu, X), contract(hidden, G)
            g_gu = part_gu if g_gu is None else g_gu + part_gu
            g_d = part_d if g_d is None else g_d + part_d

        def cut_blocks(parts):
            return nest([p[i * half : (i + 1) * half] for p in parts for i in range(na * nz)])

        da2 = scatter(cut_blocks(da2_parts))
        y = scatter(cut_blocks(y_parts))

        def pair_sum(g):
            return g[:units] + shift(g[units : 2 * units], "t")

        grad_w_gate, grad_w_up, grad_w_down = pair_sum(g_gu[:padded]), pair_sum(g_gu[padded:]), pair_sum(g_d)
        block_out = rejoin(h + y)

        sum_gain2 = jnp.sum(da2 * u2, axis=0)
        e2 = da2 * gain2
        dh = go_own.astype(F32) + inv2 * (e2 - u2 * jnp.mean(e2 * u2, axis=1, keepdims=True))
        dattn = rejoin(dh.astype(BF))
        g_out = contract(o_rel, dattn)
        grad_w_out = scatter(nest([g_out[i * no : (i + 1) * no] for i in range(n_dp)]))
        do_rel = dot_t(dattn, wo_rel).astype(BF)
        do6 = by_head(dot_t(do_rel, order_out).astype(BF), heads)

        dprob = dot_t(do6, vr)
        ds = (prob * (dprob - jnp.sum(prob * dprob, axis=1, keepdims=True))).astype(BF)
        dq6 = unrotate(dot(ds, kr) * scale, cos_all, sin_all).astype(BF)
        dk = unrotate(contract(ds, qr) * scale, cosine, sine).astype(BF)
        dv = contract(prob_low, do6).astype(BF)
        dqkv = jnp.concatenate([side_by_side(dq6, heads, rows), dk, dv], axis=1)
        sum_bias = jnp.sum(dqkv, axis=0, dtype=F32)
        d_rel = dot(dqkv, order_qkv).astype(BF)
        theirs = shift(dot(other_of(d_rel), w_rel), "t")
        da1 = dot(mine_of(d_rel), w_rel) + theirs
        u1_mine = mine_of(u1)
        sum_gain1 = jnp.sum(da1 * u1_mine, axis=0)
        e1 = da1 * gain1
        dx = dh + mine_of(inv1) * (e1 - u1_mine * jnp.mean(e1 * u1_mine, axis=1, keepdims=True))
        grad_in = rejoin(dx)

        g_qkv = contract(d_rel, a1)
        packed = jnp.concatenate(
            [
                sum_gain1.reshape(n_dp, ng),
                sum_gain2.reshape(n_dp, ng),
                sum_bias[:q_all].reshape(n_dp, nq),
                sum_bias[q_all + k_all :].reshape(n_dp, nv),
                jnp.broadcast_to(sum_bias[q_all : q_all + k_all][None], (n_dp, k_all)),
            ],
            axis=1,
        )
        packed = lax.dot_general(
            order_small.astype(F32), packed, (((0,), (0,)), ((), ())),
            precision=lax.Precision.HIGHEST, preferred_element_type=F32,
        )
        g_blocks = nest([g_qkv[i * n_qkv : (i + 1) * n_qkv] for i in range(n_dp)])
        g_sum = scatter(g_blocks)
        s_sum = packed_sum(packed, ring_f32)
        s_own = s_sum[0]
        gains = s_own[: 2 * ng] + shift(s_own[: 2 * ng], "t")
        return (
            block_out,
            grad_in,
            gains[:ng],
            g_sum[:nq],
            s_own[2 * ng : 2 * ng + nq],
            g_sum[nq : nq + nk],
            s_own[2 * ng + nq + nv :],
            g_sum[nq + nk :],
            s_own[2 * ng + nq : 2 * ng + nq + nv],
            grad_w_out,
            gains[ng:],
            grad_w_gate,
            grad_w_up,
            grad_w_down,
        )

    def ring_f32(parts, name):
        total = parts[1]
        for r in range(2, len(parts) + 1):
            total = shift(total, name) + parts[r % len(parts)]
        return total

    def packed_sum(packed, ring):
        n = packed.shape[1]
        p = packed.reshape(nb, na * nz, n)
        p = ring([p[r] for r in range(nb)], "b") if nb > 1 else p[0]
        p = p.reshape(na, nz, n)
        p = ring([p[r] for r in range(na)], "a") if na > 1 else p[0]
        return ring([p[r : r + 1] for r in range(nz)], "z")

    return shards


def solution(mesh):
    n_dp = mesh.shape["dp"]
    both = ("tensor", "dp")
    in_specs = (
        P("dp", None), P("dp", None), P("dp"), P(both, None), P(both), P(both, None), P(both), P(both, None),
        P(both), P(both, None), P("dp"), P(both, None), P(both, None), P(both, None), P("dp", None),
    )
    out_specs = (
        P("dp", None), P("dp", None), P("dp"), P(both, None), P(both), P(both, None), P("tensor"), P(both, None),
        P(both), P(both, None), P("dp"), P(both, None), P(both, None), P(both, None),
    )
    return jax.shard_map(build(n_dp), mesh=mesh, in_specs=in_specs, out_specs=out_specs, check_vma=False)
```
